32 devices in a mesh: group: 2 (over y), tensor: 4 (over z), dp: 4 (over x, core).
Axes of the slice: x: 2, y: 2, z: 4, core: 2. Of those that a mesh axis runs over, the one named last changes fastest.
Arguments:
- tokens: bfloat16 [2048, 4096], P(('group', 'dp'), 'tensor'), parts along dimension 0, may hold values from -6 to 6
- gate_weight: bfloat16 [4096, 15360], P('dp', 'tensor'), may hold values from -0.09375 to 0.09375
- up_weight: bfloat16 [4096, 15360], P('dp', 'tensor'), may hold values from -0.09375 to 0.09375
- grad_hidden: bfloat16 [2048, 15360], P(('group', 'dp'), 'tensor'), parts along dimension 0, may hold values from -6 to 6
- chosen_mask: int32 [2048], P(('group', 'dp')), parts along dimension 0, may hold values 0 or 1
- rejected_mask: int32 [2048], P(('group', 'dp')), parts along dimension 0, may hold values 0 or 1
- margins: float32 [32], P(('group', 'dp')), parts along dimension 0, may hold values from -6 to 6
Outputs:
- hidden: bfloat16 [2048, 15360], P(('group', 'dp'), 'tensor'), parts along dimension 0
- grad_tokens: bfloat16 [2048, 4096], P(('group', 'dp'), 'tensor'), parts along dimension 0
- grad_gate_weight: bfloat16 [8192, 15360], P(('group', 'dp'), 'tensor'), parts along dimension 0
- grad_up_weight: bfloat16 [8192, 15360], P(('group', 'dp'), 'tensor'), parts along dimension 0
The draws below stay inside these ranges and needn't reach their ends.
There are 2 independent parts, one for each index of `group`. The reference program is written for one: setup_inputs(seed, part) draws one part's arguments, and reference() takes and returns one part's arrays. A program takes and returns all parts, laid end to end along the dimension named above; an argument that names none is the same for every part. Nothing has to cross between parts.
All inputs are finite; a program needn't handle non-finite values. No bound on the sum of `chosen_mask` or of `rejected_mask` on one device may be relied on, other than what follows from the above.
Results may differ from the reference program's by a relative error of at most 0.012.
Values may be sent and summed in bfloat16 or wider, within the bound.
No kernel may reach another device: no remote copies, remote signals or barrier semaphores. Data moves between devices by JAX's collectives and lax.ppermute only.
A program may use at most 384 MiB of HBM per device.

```python
import jax
import jax.numpy as jnp
from jax import lax

D = 4096
FF = 15360
TOK_DEV = 256
PAIR_LEN = 64
TOKENS = 1024
PAIRS = 16
N_DP = 4


def touch_ends(drawn, rng, smallest, top_value):
    longest = drawn.shape.index(max(drawn.shape))
    spots = []
    for shift in (0, 1):
        where = [jax.random.randint(jax.random.fold_in(rng, axis), (), 0, length) for axis, length in enumerate(drawn.shape)]
        where[longest] = (where[longest] + shift) % drawn.shape[longest]
        spots.append(tuple(where))
    return drawn.at[spots[0]].set(smallest).at[spots[1]].set(top_value)


def with_spikes(result, key, source, target, shards_of, factor):
    owner, partner = [(jnp.arange(result.shape[position]) // (result.shape[position] // shards_of)).reshape([-1 if axis == position else 1 for axis in range(result.ndim)]) for position in (source, target)]
    chosen = jax.random.permutation(key, shards_of)[partner]
    strong = (owner == chosen) | (owner == (partner + shards_of // 2) % shards_of)
    return jnp.where(strong, factor * result, result)


def block_levels(stream_key, dims, pieces, least, top_value):
    loudness, own = 1.0, jax.random.fold_in(stream_key, 6)
    for dim, blocks in pieces:
        draws = jnp.exp(jax.random.uniform(jax.random.fold_in(own, dim), (blocks,), jnp.float32, least / len(pieces), top_value / len(pieces)))
        loudness = loudness * jnp.repeat(draws, dims[dim] // blocks).reshape([-1 if axis == dim else 1 for axis in range(len(dims))])
    return loudness


def scatter_about(key, extent, width, limit, cuts=(), held_as=jnp.bfloat16):
    values = jax.random.normal(key, extent, jnp.float32) * width
    if len(cuts) > 0:
        values = block_levels(key, extent, cuts, -0.22, 0.18) * values
    return jnp.clip(values, min=-limit, max=limit).astype(held_as)


def heavy_noise(own_key, shape, spread, bound, pieces, heavy, kind=jnp.bfloat16):
    values = spread * jax.random.normal(own_key, shape, jnp.float32)
    if pieces:
        values = values * block_levels(own_key, shape, pieces, -0.22, 0.18)
    return jnp.clip(with_spikes(values, jax.random.fold_in(own_key, 3), *heavy), -bound, bound).astype(kind)


def setup_inputs(seed: int = 0, part: int = 0) -> dict:
    seeds = jax.random.split(jax.random.key(seed), 8)
    own_keys = jax.random.split(jax.random.fold_in(seeds[7], part), 8)
    return {
        "tokens": heavy_noise(own_keys[0], (TOKENS, D), 1.0, 6.0, ((0, 4), (1, 4)), (0, 1, 4, 2.0)),
        "gate_weight": scatter_about(seeds[1], (D, FF), D ** -0.5, 0.09375, ((0, 4), (1, 4))),
        "up_weight": scatter_about(seeds[2], (D, FF), D ** -0.5, 0.09375, ((0, 4), (1, 4))),
        "grad_hidden": scatter_about(own_keys[3], (TOKENS, FF), 1.0, 6.0, ((0, 4), (1, 4))),
        "chosen_mask": touch_ends((jax.random.randint(own_keys[4], (TOKENS,), 0, 2) < 1).astype(jnp.int32), jax.random.fold_in(own_keys[4], 1), 0, 1),
        "rejected_mask": touch_ends((jax.random.randint(own_keys[5], (TOKENS,), 0, 2) < 1).astype(jnp.int32), jax.random.fold_in(own_keys[5], 1), 0, 1),
        "margins": jnp.clip(jax.random.uniform(own_keys[6], (PAIRS,), jnp.float32, -6.0, 6.0) * block_levels(own_keys[6], (PAIRS,), ((0, 4),), -0.4, 0.0), -6.0, 6.0),
    }


dpo_beta = 0.5


def reference(tokens, gate_weight, up_weight, grad_hidden, chosen_mask, rejected_mask, margins):
    gate_proj = jnp.dot(tokens, gate_weight, preferred_element_type=jnp.float32)
    up_proj = jnp.dot(tokens, up_weight, preferred_element_type=jnp.float32)
    gate_sigmoid = jax.nn.sigmoid(gate_proj)
    hidden = (gate_proj * gate_sigmoid * up_proj).astype(jnp.bfloat16)
    pair_weight = -dpo_beta * jax.nn.sigmoid(-dpo_beta * margins)
    token_weight = jnp.broadcast_to(pair_weight[:, None], (PAIRS, PAIR_LEN)).reshape(TOKENS)
    token_weight = token_weight * (chosen_mask - rejected_mask).astype(jnp.float32)
    cotangent = token_weight[:, None] * grad_hidden.astype(jnp.float32)
    grad_gate = (cotangent * up_proj * gate_sigmoid * (1.0 + gate_proj * (1.0 - gate_sigmoid))).astype(jnp.bfloat16)
    grad_up = (cotangent * gate_proj * gate_sigmoid).astype(jnp.bfloat16)
    grad_tokens = (jnp.dot(grad_gate, gate_weight.T, preferred_element_type=jnp.float32)
                   + jnp.dot(grad_up, up_weight.T, preferred_element_type=jnp.float32)).astype(jnp.bfloat16)
    token_blocks = tokens.reshape(N_DP, TOK_DEV, D)
    gate_blocks = grad_gate.reshape(N_DP, TOK_DEV, FF)
    up_blocks = grad_up.reshape(N_DP, TOK_DEV, FF)

    def replica_terms(totals, inputs):
        block, gate_part, up_part = inputs
        gate_term = jnp.dot(block.T, gate_part, preferred_element_type=jnp.float32).astype(jnp.bfloat16)
        up_term = jnp.dot(block.T, up_part, preferred_element_type=jnp.float32).astype(jnp.bfloat16)
        gate_term = lax.optimization_barrier(gate_term)
        up_term = lax.optimization_barrier(up_term)
        return (totals[0] + gate_term.astype(jnp.float32), totals[1] + up_term.astype(jnp.float32)), None

    zero_sum = jnp.zeros((D, FF), jnp.float32)
    totals, unused = lax.scan(replica_terms, (zero_sum, zero_sum), (token_blocks, gate_blocks, up_blocks))
    return (hidden, grad_tokens, totals[0].astype(jnp.bfloat16), totals[1].astype(jnp.bfloat16))
```

```python
import jax
import jax.numpy as jnp
from jax import lax
from jax.sharding import PartitionSpec as P

PAIR_LEN = 64
dpo_beta = 0.5
CORES = 2
PIECES = 4
bf16 = jnp.bfloat16
f32 = jnp.float32


def token_route(n_tensor, n_dp):
    n_x = n_dp // CORES
    run = n_tensor // n_x
    pairs = []
    for t in range(n_tensor):
        for d in range(n_dp):
            x_src, c = divmod(d, CORES)
            x_dst, f = divmod(t, run)
            f_rel = (f - c * (run // CORES)) % run
            x_rel = (x_src - x_dst) % n_x
            pairs.append((t * n_dp + d, (x_rel * run + f_rel) * n_dp + x_dst * CORES + c))
    return pairs


def make_local(n_tensor, n_dp):
    n_x = n_dp // CORES
    run = n_tensor // n_x
    half = run // CORES
    route = token_route(n_tensor, n_dp)
    route_back = [(b, a) for a, b in route]
    core_swap = [(d, d ^ 1) for d in range(n_dp)]
    contract_last = (((1,), (1,)), ((), ()))
    contract_first = (((0,), (0,)), ((), ()))

    def x_shift(s):
        return [(d, (d + CORES * s) % n_dp) for d in range(n_dp)]

    def dot(a, b):
        return jnp.dot(a, b, preferred_element_type=f32)

    def local(tokens, gate_weight, up_weight, grad_hidden, chosen_mask, rejected_mask, margins):
        tok_rows, feat = tokens.shape
        own_feat, width = gate_weight.shape
        rows = tok_rows // PIECES
        gate_far = lax.ppermute(gate_weight, "dp", core_swap)
        up_far = lax.ppermute(up_weight, "dp", core_swap)
        pair_weight = -dpo_beta * jax.nn.sigmoid(-dpo_beta * margins)
        token_weight = jnp.broadcast_to(pair_weight[:, None], (margins.shape[0], PAIR_LEN)).reshape(tok_rows)
        token_weight = token_weight * (chosen_mask - rejected_mask).astype(f32)

        near_toks, far_toks, grads_all, hidden_all, out_tokens = [], [], [], [], []
        for q in range(PIECES):
            part = slice(q * rows, (q + 1) * rows)
            routed = lax.ppermute(tokens[part], ("tensor", "dp"), route)
            blocks = lax.all_gather(routed, "tensor", axis=0, tiled=False)
            blocks = blocks.reshape(n_x, CORES, half, rows, feat).transpose(1, 0, 3, 2, 4)
            blocks = blocks.reshape(CORES, n_x * rows, own_feat)
            near, far = blocks[0], blocks[1]
            gate_part = dot(near, gate_weight) + dot(far, gate_far)
            up_part = dot(near, up_weight) + dot(far, up_far)
            gate_acc, up_acc = gate_part[:rows], up_part[:rows]
            for s in range(1, n_x):
                sent = jnp.concatenate(
                    [gate_part[s * rows:(s + 1) * rows], up_part[s * rows:(s + 1) * rows]], axis=0
                ).astype(bf16)
                got = lax.ppermute(sent, "dp", x_shift(s)).astype(f32)
                gate_acc = gate_acc + got[:rows]
                up_acc = up_acc + got[rows:]
            sig = jax.nn.sigmoid(gate_acc)
            hidden_all.append((gate_acc * sig * up_acc).astype(bf16))
            cot = token_weight[part][:, None] * grad_hidden[part].astype(f32)
            grad_gate = (cot * up_acc * sig * (1.0 + gate_acc * (1.0 - sig))).astype(bf16)
            grad_up = (cot * gate_acc * sig).astype(bf16)
            own = jnp.stack([grad_gate, grad_up])
            grads = [own] + [lax.ppermute(own, "dp", x_shift(-s)) for s in range(1, n_x)]
            grads = jnp.concatenate(grads, axis=1)
            gg, gu = grads[0], grads[1]
            tg_near = lax.dot_general(gg, gate_weight, contract_last, preferred_element_type=f32) + lax.dot_general(
                gu, up_weight, contract_last, preferred_element_type=f32)
            tg_far = lax.dot_general(gg, gate_far, contract_last, preferred_element_type=f32) + lax.dot_general(
                gu, up_far, contract_last, preferred_element_type=f32)
            tg = jnp.stack([tg_near, tg_far]).astype(bf16)
            tg = tg.reshape(CORES, n_x, rows, half, feat).transpose(1, 0, 3, 2, 4).reshape(n_tensor * rows, feat)
            summed = lax.psum_scatter(tg, "tensor", scatter_dimension=0, tiled=True)
            out_tokens.append(lax.ppermute(summed, ("tensor", "dp"), route_back))
            near_toks.append(near)
            far_toks.append(far)
            grads_all.append(grads)
        near_all = jnp.concatenate(near_toks, axis=0)
        far_all = lax.ppermute(jnp.concatenate(far_toks, axis=0), "dp", core_swap)
        toks = jnp.concatenate([near_all, far_all], axis=0)
        grads = jnp.concatenate(grads_all, axis=1)
        grads = jnp.concatenate([grads, lax.ppermute(grads, "dp", core_swap)], axis=1)
        d_gate = lax.dot_general(toks, grads[0], contract_first, preferred_element_type=f32).astype(bf16)
        d_up = lax.dot_general(toks, grads[1], contract_first, preferred_element_type=f32).astype(bf16)
        return (jnp.concatenate(hidden_all, axis=0), jnp.concatenate(out_tokens, axis=0), d_gate, d_up)

    return local


def solution(mesh):
    in_specs = (
        P(("group", "dp"), "tensor"),
        P("dp", "tensor"),
        P("dp", "tensor"),
        P(("group", "dp"), "tensor"),
        P(("group", "dp")),
        P(("group", "dp")),
        P(("group", "dp")),
    )
    out_specs = (P(("group", "dp"), "tensor"),) * 4
    local = make_local(mesh.shape["tensor"], mesh.shape["dp"])
    return jax.shard_map(local, mesh=mesh, in_specs=in_specs, out_specs=out_specs, check_vma=False)
```

```python
import jax
import jax.numpy as jnp
from jax import lax
from jax.experimental import pallas as pl
from jax.experimental.pallas import tpu as pltpu
from jax.sharding import PartitionSpec as P

PAIR_LEN = 64
dpo_beta = 0.5
CORES = 2
SIXTEENTHS = (2, 5, 4, 5)
LAST_SPLIT = (5,)
FINAL = ((0, 4), (4, 1))
BLOCK = 768
SHORT = 4
bf16 = jnp.bfloat16
f32 = jnp.float32
ANY = pl.BlockSpec(memory_space=pl.ANY)
SMEM = pl.BlockSpec(memory_space=pltpu.SMEM)
VMEM = pl.BlockSpec(memory_space=pltpu.VMEM)


def token_route(n_tensor, n_dp):
    n_x = n_dp // CORES
    run = n_tensor // n_x
    pairs = []
    for t in range(n_tensor):
        for d in range(n_dp):
            x_src, c = divmod(d, CORES)
            x_dst, f = divmod(t, run)
            f_rel = (f - c * (run // CORES)) % run
            x_rel = (x_src - x_dst) % n_x
            pairs.append((t * n_dp + d, (x_rel * run + f_rel) * n_dp + x_dst * CORES + c))
    return pairs


def dot(a, b):
    return jnp.dot(a, b, preferred_element_type=f32)


def dot_nt(a, b):
    return lax.dot_general(a, b, (((1,), (1,)), ((), ())), preferred_element_type=f32)


def call(body, grid, ins, outs, deps=(), scratch=(), aliases=None, mib=48, flops=1, nbytes=1):
    n_in, n_dep = len(ins), len(deps)

    def wrapped(*refs):
        body(*refs[:n_in], *refs[n_in + n_dep:])

    return pl.pallas_call(
        wrapped,
        grid=grid,
        in_specs=[spec for _, spec in ins] + [ANY] * n_dep,
        out_specs=[spec for _, _, spec in outs],
        out_shape=[jax.ShapeDtypeStruct(shape, dtype) for shape, dtype, _ in outs],
        scratch_shapes=list(scratch),
        input_output_aliases=aliases or {},
        compiler_params=pltpu.CompilerParams(
            dimension_semantics=("arbitrary",) * len(grid), vmem_limit_bytes=mib << 20),
        cost_estimate=pl.CostEstimate(flops=flops, transcendentals=0, bytes_accessed=nbytes),
    )(*[a for a, _ in ins], *deps)


def forward_tile(near, far, weights, deps, n_x, block):
    rows = near.shape[0] // n_x
    feat, width = weights[0][0].shape
    n = len(weights)

    def body(near_ref, far_ref, *refs):
        own_ref, send_ref = refs[2 * n:]
        for m in range(n):
            part = dot(near_ref[...], refs[2 * m][...]) + dot(far_ref[...], refs[2 * m + 1][...])
            own_ref[m] = part[:rows]
            for s in range(1, n_x):
                send_ref[s - 1, m] = part[s * rows:(s + 1) * rows].astype(bf16)

    w_spec = pl.BlockSpec((feat, block), lambda i: (0, i))
    full = pl.BlockSpec(near.shape, lambda i: (0, 0))
    return call(
        body, (width // block,),
        [(near, full), (far, full)] + [(w, w_spec) for pair in weights for w in pair],
        [((n, rows, width), f32, pl.BlockSpec((n, rows, block), lambda i: (0, 0, i))),
         ((n_x - 1, n, rows, width), bf16, pl.BlockSpec((n_x - 1, n, rows, block), lambda i: (0, 0, 0, i)))],
        deps, flops=4 * n * n_x * rows * feat * width, nbytes=4 * n * feat * width)


def gate_tile(gate_terms, up_terms, grad_hidden, token_weight, deps, block, row_start, start, count):
    rows = token_weight.shape[0]
    n = len(gate_terms)

    def body(*refs):
        gh_ref, tw_ref, hidden_ref, mine_ref = refs[2 * n:]
        gate, up = refs[0][0], refs[n][0]
        for k in range(1, n):
            gate = gate + refs[k][0].astype(f32)
            up = up + refs[n + k][0].astype(f32)
        sig = 1.0 / (1.0 + jnp.exp(-gate))
        hidden_ref[...] = (gate * sig * up).astype(bf16)
        cot = tw_ref[...] * gh_ref[...].astype(f32)
        mine_ref[0] = (cot * up * sig * (1.0 + gate * (1.0 - sig))).astype(bf16)
        mine_ref[1] = (cot * gate * sig).astype(bf16)

    if row_start % rows:
        grad_hidden = grad_hidden[row_start:row_start + rows]
        row_start = 0
    ins = [(a, pl.BlockSpec((1, rows, block), lambda i, m=m: (m, 0, start + i))) for a, m in gate_terms + up_terms]
    ins += [(grad_hidden, pl.BlockSpec((rows, block), lambda i: (row_start // rows, start + i))),
            (token_weight, pl.BlockSpec((rows, 1), lambda i: (0, 0)))]
    cols = count * block
    return call(
        body, (count,), ins,
        [((rows, cols), bf16, pl.BlockSpec((rows, block), lambda i: (0, i))),
         ((2, rows, cols), bf16, pl.BlockSpec((2, rows, block), lambda i: (0, 0, i)))],
        deps, mib=32, flops=40 * rows * cols, nbytes=20 * rows * cols)


def token_grad_tile(grads, weights, before, deps, z, n_x, n_tensor, block, start, count, final, split):
    feat = weights[0].shape[0]
    flat = [g for per_x in grads for g in per_x]
    n = len(flat)
    rows = sum(g.shape[1] for g in grads[0])
    total = rows * n_x
    wide = n_x * feat * CORES // n_tensor
    per_core = feat // wide
    split = split and final and n_tensor == SHORT

    def body(z_ref, *refs):
        g_refs = refs[:n]
        ws = refs[n:n + 4]
        rest = refs[n + 4:]
        if before is not None:
            before_ref, rest = rest[0], rest[1:]
        both_ref, *out_refs, acc_ref = rest
        i = pl.program_id(0)
        gg = jnp.concatenate([r[0] for r in g_refs], axis=0)
        gu = jnp.concatenate([r[1] for r in g_refs], axis=0)
        both_ref[0] = gg
        both_ref[1] = gu
        near = dot_nt(gg, ws[0][...]) + dot_nt(gu, ws[1][...])
        far = dot_nt(gg, ws[2][...]) + dot_nt(gu, ws[3][...])

        @pl.when(i == 0)
        def _():
            if before is None:
                acc_ref[0] = near
                acc_ref[1] = far
            else:
                acc_ref[0] = before_ref[0] + near
                acc_ref[1] = before_ref[1] + far

        @pl.when(i > 0)
        def _():
            acc_ref[0] += near
            acc_ref[1] += far

        @pl.when(i == count - 1)
        def _():
            if not final:
                out_refs[0][...] = acc_ref[...]
                return
            sums = [acc_ref[c] for c in range(CORES)]
            for x in range(n_x):
                for c in range(CORES):
                    value = sums[c][x * rows:(x + 1) * rows]
                    if not split:
                        out_refs[0][x, c] = value.astype(bf16)
                        continue
                    for k in range(per_core):
                        b = (x * CORES + c) * per_core + k
                        part = value[:, k * wide:(k + 1) * wide]
                        for s in range(n_tensor):
                            @pl.when(z_ref[0] == b ^ s)
                            def _():
                                if s < 2:
                                    out_refs[0][s] = part
                                else:
                                    out_refs[1][s - 2] = part.astype(bf16)

    w_spec = pl.BlockSpec((feat, block), lambda i: (0, start + i))
    ins = [(z, SMEM)] + [(g, pl.BlockSpec((2, g.shape[1], block), lambda i: (0, 0, i))) for g in flat]
    ins += [(w, w_spec) for w in weights]

    def fixed(shape, dtype):
        return (shape, dtype, pl.BlockSpec(shape, lambda i: (0,) * len(shape)))

    acc_shape = (CORES, total, feat)
    if before is not None:
        ins.append((before, fixed(acc_shape, f32)[2]))
    cols = count * block
    outs = [((2, total, cols), bf16, pl.BlockSpec((2, total, block), lambda i: (0, 0, i)))]
    if split:
        outs += [fixed((2, rows, wide), f32), fixed((2, rows, wide), bf16)]
    elif final:
        outs += [fixed((n_x, CORES, rows, feat), bf16)]
    else:
        outs += [fixed(acc_shape, f32)]
    return call(
        body, (count,), ins, outs, deps, scratch=[pltpu.VMEM(acc_shape, f32)], mib=58,
        flops=8 * total * feat * cols, nbytes=8 * feat * cols)


def weight_grad_tile(toks_t, width, block, deps, segments, outs=None):
    feat, n_tok = toks_t[0].shape
    for (start, count), sides in segments:
        parts = [p for side in sides for p in side]
        n, n_side = len(parts), len(sides[0])

        def body(*refs):
            out_refs = refs[-2:]
            for m in range(2):
                total = 0.0
                for c in range(CORES):
                    part = refs[CORES + c * n_side:CORES + (c + 1) * n_side]
                    total = total + dot(refs[c][...], jnp.concatenate([r[m] for r in part], axis=0))
                out_refs[m][...] = total.astype(bf16)

        ins = [(t, pl.BlockSpec(t.shape, lambda i: (0, 0))) for t in toks_t]
        for g, off in parts:
            ins.append((g, pl.BlockSpec((2, g.shape[1], block), lambda i, off=off: (0, 0, off + i))))
        aliases = {}
        if outs is not None:
            aliases = {len(ins): 0, len(ins) + 1: 1}
            ins += [(o, ANY) for o in outs]
        spec = pl.BlockSpec((feat, block), lambda i, start=start: (0, start + i))
        cols = count * block
        outs = call(
            body, (count,), ins, [((feat, width), bf16, spec)] * 2, deps, aliases=aliases,
            flops=8 * feat * n_tok * cols, nbytes=4 * (feat + 2 * n_tok) * cols)
        deps = ()
    return outs


def order_tokens(groups, n_x, deps):
    pieces = [p for group in groups for p in group]
    feat = pieces[0][0].shape[1]
    n_rows = sum(p[0].shape[0] for p in pieces)
    n = len(pieces)

    def body(*refs):
        near_ref, far_ref = refs[2 * n:]
        at, base = 0, 0
        for group in groups:
            for x in range(n_x):
                for k, (a, _) in enumerate(group):
                    rows = a.shape[0] // n_x
                    near, far = refs[base + k], refs[n + base + k]
                    near_ref[:, at:at + rows] = near[x * rows:(x + 1) * rows].astype(f32).T.astype(bf16)
                    far_ref[at:at + rows] = far[x * rows:(x + 1) * rows]
                    at += rows
            base += len(group)

    return call(
        body, (), [(p[k], VMEM) for k in range(2) for p in pieces],
        [((feat, n_rows), bf16, VMEM), ((n_rows, feat), bf16, VMEM)], deps, mib=32)


def transposed(x):
    def body(x_ref, o_ref):
        o_ref[...] = x_ref[...].astype(f32).T.astype(bf16)

    return call(body, (), [(x, VMEM)], [(x.shape[::-1], bf16, VMEM)], mib=32)[0]


def arrange_column(pairs, z, n_x, first, rows):
    feat = pairs[0].shape[2]
    n_tensor = 2 * len(pairs)
    half = n_tensor // n_x // CORES
    shape = (n_x * rows, half * feat)

    def body(z_ref, *refs):
        outs = refs[len(pairs):]
        for s in range(n_tensor):
            for b in range(n_tensor):
                x, f = divmod(b, half * CORES)
                core, k = divmod(f, half)

                @pl.when(z_ref[0] == b ^ s)
                def _():
                    outs[core][x * rows:(x + 1) * rows, k * feat:(k + 1) * feat] = refs[s // 2][s % 2, first:first + rows]

    return call(body, (), [(z, SMEM)] + [(p, VMEM) for p in pairs], [(shape, bf16, VMEM)] * CORES, mib=16)


def after(x, deps):
    def body(x_ref, o_ref):
        o_ref[...] = x_ref[...]

    return call(body, (), [(x, VMEM)], [(x.shape, x.dtype, VMEM)], deps, mib=16)[0]


def make_local(n_tensor, n_dp):
    n_x = n_dp // CORES
    run = n_tensor // n_x
    half = run // CORES
    route = token_route(n_tensor, n_dp)
    route_back = [(b, a) for a, b in route]
    core_swap = [(d, d ^ 1) for d in range(n_dp)]

    def x_shift(s):
        return [(d, (d + CORES * s) % n_dp) for d in range(n_dp)]

    def z_flip(a, k):
        return lax.ppermute(a, "tensor", [(t, t ^ k) for t in range(n_tensor)])

    def swap(a):
        return lax.ppermute(a, "dp", core_swap)

    def send_home(summed):
        return lax.ppermute(summed, ("tensor", "dp"), route_back)

    def gather_column(block, z, pieces):
        if n_tensor != SHORT:
            got = lax.all_gather(block, "tensor", axis=0, tiled=False)
            result = []
            for first, rows in pieces:
                part = got[:, first:first + rows].reshape(n_x, CORES, half, rows, -1).transpose(1, 0, 3, 2, 4)
                part = part.reshape(CORES, n_x * rows, -1)
                result.append((part[0], part[1]))
            return result
        pair = jnp.stack([block, z_flip(block, 1)])
        pairs = [pair, z_flip(pair, 2)]
        return [arrange_column(pairs, z, n_x, first, rows) for first, rows in pieces]

    def reduce_column(blocks):
        blocks = jnp.concatenate(blocks, axis=2)
        rows, feat = blocks.shape[2], blocks.shape[3] // half
        blocks = blocks.reshape(n_x, CORES, rows, half, feat).transpose(0, 1, 3, 2, 4)
        return lax.psum_scatter(
            blocks.reshape(n_tensor, rows, feat), "tensor", scatter_dimension=0, tiled=False)

    def local(tokens, gate_weight, up_weight, grad_hidden, chosen_mask, rejected_mask, margins):
        tok_rows = tokens.shape[0]
        width = gate_weight.shape[1]
        block = BLOCK if width % BLOCK == 0 else width
        n_blocks = width // block
        sizes = [tok_rows * k // 16 for k in SIXTEENTHS]
        begins = [sum(sizes[:q]) for q in range(4)]
        last_split = LAST_SPLIT if sum(LAST_SPLIT) == n_blocks else (n_blocks,)
        pair_weight = -dpo_beta * jax.nn.sigmoid(-dpo_beta * margins)
        token_weight = jnp.broadcast_to(pair_weight[:, None], (margins.shape[0], PAIR_LEN)).reshape(tok_rows)
        token_weight = (token_weight * (chosen_mask - rejected_mask).astype(f32))[:, None]
        z = lax.axis_index("tensor").reshape(1)

        def forward(near_far, mats, deps):
            own, send = forward_tile(*near_far, mats, deps, n_x, block)
            return own, [lax.ppermute(send[s - 1], "dp", x_shift(s)) for s in range(1, n_x)]

        def gates(q, terms, deps, start=0, count=n_blocks):
            return gate_tile(*terms, grad_hidden, token_weight[begins[q]:begins[q] + sizes[q]], deps, block,
                             begins[q], start, count)

        def both_terms(own, got):
            return [[(a, m) for a in [own] + got] for m in range(2)]

        def exchange(mine):
            return [mine] + [lax.ppermute(mine, "dp", x_shift(-s)) for s in range(1, n_x)]

        def rows_of(q, n=1):
            return tokens[begins[q]:begins[q + n - 1] + sizes[q + n - 1]]

        def routed(a):
            return lax.ppermute(a, ("tensor", "dp"), route)

        column = n_tensor == SHORT
        mats = [(gate_weight, swap(gate_weight)), (up_weight, swap(up_weight))]
        weights = [pair[c] for c in range(CORES) for pair in mats]
        t0, t1 = gather_column(routed(rows_of(0, 2)), z, [(0, sizes[0]), (sizes[0], sizes[1])])
        r23 = routed(after(rows_of(2, 2), [t0[0]]))
        own0, got0 = forward(t0, mats, [])
        t2, = gather_column(after(r23[:sizes[2]], [own0]), z, [(0, sizes[2])])
        hidden0, mine0 = gates(0, both_terms(own0, got0), [])
        grads0 = exchange(mine0)
        own1, got1 = forward(t1, mats, [mine0])
        own2, got2 = forward(t2, mats, [own1] + grads0[1:])
        t3, = gather_column(after(r23[sizes[2]:], [t2[0]]), z, [(0, sizes[3])])
        hidden1, mine1 = gates(1, both_terms(own1, got1), [own2])
        grads1 = exchange(mine1)

        def token_grads(grads, deps, before=None, start=0, count=n_blocks, final=True, split=False):
            return token_grad_tile(
                [[g] for g in grads], weights, before, deps, z, n_x, n_tensor, block, start, count, final, split)

        both0, *sums0 = token_grads(grads0, [mine1])
        swapped0 = swap(both0)
        near_t, far_order = order_tokens([[t0], [t1], [t2], [t3]], n_x, [both0])
        far_t = transposed(swap(far_order))
        own3, got3 = forward(t3, mats, [near_t] + got2)
        hidden2, mine2 = gates(2, both_terms(own2, got2), [own3] + grads1[1:])
        grads2 = exchange(mine2)
        hidden3, grads3 = [], []
        deps = [mine2]
        start = 0
        for count in last_split:
            h, mine = gates(3, both_terms(own3, got3), deps, start, count)
            hidden3.append(h)
            grads3.append((exchange(mine), start, count))
            deps = [mine]
            start += count
        deps += [far_t, swapped0]
        both1, *sums1 = token_grads(grads1, deps)
        swapped1 = swap(both1)
        deps = [both1]
        both2, *sums2 = token_grads(grads2, deps)
        swapped2 = swap(both2)
        done = [reduce_column([sums0[0], sums1[0]])]
        deps = [both2]
        before = None
        both3s = []
        for k, (grads, start, count) in enumerate(grads3):
            both3, *sums3 = token_grads(grads, deps, before, start, count, k == len(grads3) - 1)
            before = sums3[0]
            deps = [both3]
            both3s.append((both3, swap(both3), start, count))
        segments = []
        for start, count in FINAL if column and sum(c for _, c in FINAL) == n_blocks else [(0, n_blocks)]:
            for both3, swapped3, at, n in both3s:
                first, stop = max(start, at), min(start + count, at + n)
                if first < stop:
                    segments.append(((first, stop - first), [
                        [(both0, first), (both1, first), (both2, first), (both3, first - at)],
                        [(swapped0, first), (swapped1, first), (swapped2, first), (swapped3, first - at)]]))
        outs = weight_grad_tile([near_t, far_t], width, block, deps + done, segments[:1])
        done.append(reduce_column([sums2[0], sums3[0]]))
        done[0] = after(done[0], [outs[0]])
        outs = weight_grad_tile([near_t, far_t], width, block, [], segments[1:], outs)
        out = send_home(jnp.concatenate(done, axis=0))
        hidden = jnp.concatenate([hidden0, hidden1, hidden2, jnp.concatenate(hidden3, axis=1)], axis=0)
        return (hidden, out, outs[0], outs[1])

    return local


def solution(mesh):
    in_specs = (
        P(("group", "dp"), "tensor"),
        P("dp", "tensor"),
        P("dp", "tensor"),
        P(("group", "dp"), "tensor"),
        P(("group", "dp")),
        P(("group", "dp")),
        P(("group", "dp")),
    )
    out_specs = (P(("group", "dp"), "tensor"),) * 4
    local = make_local(mesh.shape["tensor"], mesh.shape["dp"])
    return jax.shard_map(local, mesh=mesh, in_specs=in_specs, out_specs=out_specs, check_vma=False)
```

```python
import jax
import jax.numpy as jnp
from jax import lax
from jax.experimental import pallas as pl
from jax.experimental.pallas import tpu as pltpu
from jax.sharding import PartitionSpec as P

PAIR_LEN = 64
dpo_beta = 0.5
CORES = 2
SIXTEENTHS = (2, 5, 4, 5)
LAST_SPLIT = (5,)
FINAL = ((0, 4), (4, 1))
BLOCK = 768
SHORT = 4
bf16 = jnp.bfloat16
f32 = jnp.float32
ANY = pl.BlockSpec(memory_space=pl.ANY)
SMEM = pl.BlockSpec(memory_space=pltpu.SMEM)
VMEM = pl.BlockSpec(memory_space=pltpu.VMEM)


def token_route(n_tensor, n_dp):
    n_x = n_dp // CORES
    run = n_tensor // n_x
    pairs = []
    for t in range(n_tensor):
        for d in range(n_dp):
            x_src, c = divmod(d, CORES)
            x_dst, f = divmod(t, run)
            f_rel = (f - c * (run // CORES)) % run
            x_rel = (x_src - x_dst) % n_x
            pairs.append((t * n_dp + d, (x_rel * run + f_rel) * n_dp + x_dst * CORES + c))
    return pairs


def dot(a, b):
    return jnp.dot(a, b, preferred_element_type=f32)


def dot_nt(a, b):
    return lax.dot_general(a, b, (((1,), (1,)), ((), ())), preferred_element_type=f32)


def call(body, grid, ins, outs, deps=(), scratch=(), aliases=None, mib=48, flops=1, nbytes=1):
    n_in, n_dep = len(ins), len(deps)

    def wrapped(*refs):
        body(*refs[:n_in], *refs[n_in + n_dep:])

    return pl.pallas_call(
        wrapped,
        grid=grid,
        in_specs=[spec for _, spec in ins] + [ANY] * n_dep,
        out_specs=[spec for _, _, spec in outs],
        out_shape=[jax.ShapeDtypeStruct(shape, dtype) for shape, dtype, _ in outs],
        scratch_shapes=list(scratch),
        input_output_aliases=aliases or {},
        compiler_params=pltpu.CompilerParams(
            dimension_semantics=("arbitrary",) * len(grid), vmem_limit_bytes=mib << 20),
        cost_estimate=pl.CostEstimate(flops=flops, transcendentals=0, bytes_accessed=nbytes),
    )(*[a for a, _ in ins], *deps)


def forward_tile(near, far, weights, deps, n_x, block):
    rows = near.shape[0] // n_x
    feat, width = weights[0][0].shape
    n = len(weights)

    def body(near_ref, far_ref, *refs):
        own_ref, send_ref = refs[2 * n:]
        for m in range(n):
            part = dot(near_ref[...], refs[2 * m][...]) + dot(far_ref[...], refs[2 * m + 1][...])
            own_ref[m] = part[:rows]
            for s in range(1, n_x):
                send_ref[s - 1, m] = part[s * rows:(s + 1) * rows].astype(bf16)

    w_spec = pl.BlockSpec((feat, block), lambda i: (0, i))
    full = pl.BlockSpec(near.shape, lambda i: (0, 0))
    return call(
        body, (width // block,),
        [(near, full), (far, full)] + [(w, w_spec) for pair in weights for w in pair],
        [((n, rows, width), f32, pl.BlockSpec((n, rows, block), lambda i: (0, 0, i))),
         ((n_x - 1, n, rows, width), bf16, pl.BlockSpec((n_x - 1, n, rows, block), lambda i: (0, 0, 0, i)))],
        deps, flops=4 * n * n_x * rows * feat * width, nbytes=4 * n * feat * width)


def gate_tile(gate_terms, up_terms, grad_hidden, token_weight, deps, block, row_start, start, count):
    rows = token_weight.shape[0]
    n = len(gate_terms)

    def body(*refs):
        gh_ref, tw_ref, hidden_ref, mine_ref = refs[2 * n:]
        gate, up = refs[0][0], refs[n][0]
        for k in range(1, n):
            gate = gate + refs[k][0].astype(f32)
            up = up + refs[n + k][0].astype(f32)
        sig = 1.0 / (1.0 + jnp.exp(-gate))
        hidden_ref[...] = (gate * sig * up).astype(bf16)
        cot = tw_ref[...] * gh_ref[...].astype(f32)
        mine_ref[0] = (cot * up * sig * (1.0 + gate * (1.0 - sig))).astype(bf16)
        mine_ref[1] = (cot * gate * sig).astype(bf16)

    if row_start % rows:
        grad_hidden = grad_hidden[row_start:row_start + rows]
        row_start = 0
    ins = [(a, pl.BlockSpec((1, rows, block), lambda i, m=m: (m, 0, start + i))) for a, m in gate_terms + up_terms]
    ins += [(grad_hidden, pl.BlockSpec((rows, block), lambda i: (row_start // rows, start + i))),
            (token_weight, pl.BlockSpec((rows, 1), lambda i: (0, 0)))]
    cols = count * block
    return call(
        body, (count,), ins,
        [((rows, cols), bf16, pl.BlockSpec((rows, block), lambda i: (0, i))),
         ((2, rows, cols), bf16, pl.BlockSpec((2, rows, block), lambda i: (0, 0, i)))],
        deps, mib=32, flops=40 * rows * cols, nbytes=20 * rows * cols)


def token_grad_tile(grads, weights, before, deps, z, n_x, n_tensor, block, start, count, final, split):
    feat = weights[0].shape[0]
    flat = [g for per_x in grads for g in per_x]
    n = len(flat)
    rows = sum(g.shape[1] for g in grads[0])
    total = rows * n_x
    wide = n_x * feat * CORES // n_tensor
    per_core = feat // wide
    split = split and final and n_tensor == SHORT

    def body(z_ref, *refs):
        g_refs = refs[:n]
        ws = refs[n:n + 4]
        rest = refs[n + 4:]
        if before is not None:
            before_ref, rest = rest[0], rest[1:]
        both_ref, *out_refs, acc_ref = rest
        i = pl.program_id(0)
        gg = jnp.concatenate([r[0] for r in g_refs], axis=0)
        gu = jnp.concatenate([r[1] for r in g_refs], axis=0)
        both_ref[0] = gg
        both_ref[1] = gu
        near = dot_nt(gg, ws[0][...]) + dot_nt(gu, ws[1][...])
        far = dot_nt(gg, ws[2][...]) + dot_nt(gu, ws[3][...])

        @pl.when(i == 0)
        def _():
            if before is None:
                acc_ref[0] = near
                acc_ref[1] = far
            else:
                acc_ref[0] = before_ref[0] + near
                acc_ref[1] = before_ref[1] + far

        @pl.when(i > 0)
        def _():
            acc_ref[0] += near
            acc_ref[1] += far

        @pl.when(i == count - 1)
        def _():
            if not final:
                out_refs[0][...] = acc_ref[...]
                return
            sums = [acc_ref[c] for c in range(CORES)]
            for x in range(n_x):
                for c in range(CORES):
                    value = sums[c][x * rows:(x + 1) * rows]
                    if not split:
                        out_refs[0][x, c] = value.astype(bf16)
                        continue
                    for k in range(per_core):
                        b = (x * CORES + c) * per_core + k
                        part = value[:, k * wide:(k + 1) * wide]
                        for s in range(n_tensor):
                            @pl.when(z_ref[0] == b ^ s)
                            def _():
                                if s < 2:
                                    out_refs[0][s] = part
                                else:
                                    out_refs[1][s - 2] = part.astype(bf16)

    w_spec = pl.BlockSpec((feat, block), lambda i: (0, start + i))
    ins = [(z, SMEM)] + [(g, pl.BlockSpec((2, g.shape[1], block), lambda i: (0, 0, i))) for g in flat]
    ins += [(w, w_spec) for w in weights]

    def fixed(shape, dtype):
        return (shape, dtype, pl.BlockSpec(shape, lambda i: (0,) * len(shape)))

    acc_shape = (CORES, total, feat)
    if before is not None:
        ins.append((before, fixed(acc_shape, f32)[2]))
    cols = count * block
    outs = [((2, total, cols), bf16, pl.BlockSpec((2, total, block), lambda i: (0, 0, i)))]
    if split:
        outs += [fixed((2, rows, wide), f32), fixed((2, rows, wide), bf16)]
    elif final:
        outs += [fixed((n_x, CORES, rows, feat), bf16)]
    else:
        outs += [fixed(acc_shape, f32)]
    return call(
        body, (count,), ins, outs, deps, scratch=[pltpu.VMEM(acc_shape, f32)], mib=58,
        flops=8 * total * feat * cols, nbytes=8 * feat * cols)


def weight_grad_tile(toks_t, width, block, deps, segments, outs=None):
    feat, n_tok = toks_t[0].shape
    for (start, count), sides in segments:
        parts = [p for side in sides for p in side]
        n, n_side = len(parts), len(sides[0])

        def body(*refs):
            out_refs = refs[-2:]
            for m in range(2):
                total = 0.0
                for c in range(CORES):
                    part = refs[CORES + c * n_side:CORES + (c + 1) * n_side]
                    total = total + dot(refs[c][...], jnp.concatenate([r[m] for r in part], axis=0))
                out_refs[m][...] = total.astype(bf16)

        ins = [(t, pl.BlockSpec(t.shape, lambda i: (0, 0))) for t in toks_t]
        for g, off in parts:
            ins.append((g, pl.BlockSpec((2, g.shape[1], block), lambda i, off=off: (0, 0, off + i))))
        aliases = {}
        if outs is not None:
            aliases = {len(ins): 0, len(ins) + 1: 1}
            ins += [(o, ANY) for o in outs]
        spec = pl.BlockSpec((feat, block), lambda i, start=start: (0, start + i))
        cols = count * block
        outs = call(
            body, (count,), ins, [((feat, width), bf16, spec)] * 2, deps, aliases=aliases,
            flops=8 * feat * n_tok * cols, nbytes=4 * (feat + 2 * n_tok) * cols)
        deps = ()
    return outs


def order_tokens(groups, n_x, deps):
    pieces = [p for group in groups for p in group]
    feat = pieces[0][0].shape[1]
    n_rows = sum(p[0].shape[0] for p in pieces)
    n = len(pieces)

    def body(*refs):
        near_ref, far_ref = refs[2 * n:]
        at, base = 0, 0
        for group in groups:
            for x in range(n_x):
                for k, (a, _) in enumerate(group):
                    rows = a.shape[0] // n_x
                    near, far = refs[base + k], refs[n + base + k]
                    near_ref[:, at:at + rows] = near[x * rows:(x + 1) * rows].astype(f32).T.astype(bf16)
                    far_ref[at:at + rows] = far[x * rows:(x + 1) * rows]
                    at += rows
            base += len(group)

    return call(
        body, (), [(p[k], VMEM) for k in range(2) for p in pieces],
        [((feat, n_rows), bf16, VMEM), ((n_rows, feat), bf16, VMEM)], deps, mib=32)


def transposed(x):
    def body(x_ref, o_ref):
        o_ref[...] = x_ref[...].astype(f32).T.astype(bf16)

    return call(body, (), [(x, VMEM)], [(x.shape[::-1], bf16, VMEM)], mib=32)[0]


def arrange_column(pairs, z, n_x, first, rows):
    feat = pairs[0].shape[2]
    n_tensor = 2 * len(pairs)
    half = n_tensor // n_x // CORES
    shape = (n_x * rows, half * feat)

    def body(z_ref, *refs):
        outs = refs[len(pairs):]
        for s in range(n_tensor):
            for b in range(n_tensor):
                x, f = divmod(b, half * CORES)
                core, k = divmod(f, half)

                @pl.when(z_ref[0] == b ^ s)
                def _():
                    outs[core][x * rows:(x + 1) * rows, k * feat:(k + 1) * feat] = refs[s // 2][s % 2, first:first + rows]

    return call(body, (), [(z, SMEM)] + [(p, VMEM) for p in pairs], [(shape, bf16, VMEM)] * CORES, mib=16)


def after(x, deps):
    def body(x_ref, o_ref):
        o_ref[...] = x_ref[...]

    return call(body, (), [(x, VMEM)], [(x.shape, x.dtype, VMEM)], deps, mib=16)[0]


def make_local(n_tensor, n_dp):
    n_x = n_dp // CORES
    run = n_tensor // n_x
    half = run // CORES
    route = token_route(n_tensor, n_dp)
    route_back = [(b, a) for a, b in route]
    core_swap = [(d, d ^ 1) for d in range(n_dp)]

    def x_shift(s):
        return [(d, (d + CORES * s) % n_dp) for d in range(n_dp)]

    def z_flip(a, k):
        return lax.ppermute(a, "tensor", [(t, t ^ k) for t in range(n_tensor)])

    def swap(a):
        return lax.ppermute(a, "dp", core_swap)

    def send_home(summed):
        return lax.ppermute(summed, ("tensor", "dp"), route_back)

    def gather_column(block, z, pieces):
        if n_tensor != SHORT:
            got = lax.all_gather(block, "tensor", axis=0, tiled=False)
            result = []
            for first, rows in pieces:
                part = got[:, first:first + rows].reshape(n_x, CORES, half, rows, -1).transpose(1, 0, 3, 2, 4)
                part = part.reshape(CORES, n_x * rows, -1)
                result.append((part[0], part[1]))
            return result
        pair = jnp.stack([block, z_flip(block, 1)])
        pairs = [pair, z_flip(pair, 2)]
        return [arrange_column(pairs, z, n_x, first, rows) for first, rows in pieces]

    def reduce_column(blocks):
        blocks = jnp.concatenate(blocks, axis=2)
        rows, feat = blocks.shape[2], blocks.shape[3] // half
        blocks = blocks.reshape(n_x, CORES, rows, half, feat).transpose(0, 1, 3, 2, 4)
        return lax.psum_scatter(
            blocks.reshape(n_tensor, rows, feat), "tensor", scatter_dimension=0, tiled=False)

    def local(tokens, gate_weight, up_weight, grad_hidden, chosen_mask, rejected_mask, margins):
        tok_rows = tokens.shape[0]
        width = gate_weight.shape[1]
        block = BLOCK if width % BLOCK == 0 else width
        n_blocks = width // block
        sizes = [tok_rows * k // 16 for k in SIXTEENTHS]
        begins = [sum(sizes[:q]) for q in range(4)]
        last_split = LAST_SPLIT if sum(LAST_SPLIT) == n_blocks else (n_blocks,)
        pair_weight = -dpo_beta * jax.nn.sigmoid(-dpo_beta * margins)
        token_weight = jnp.broadcast_to(pair_weight[:, None], (margins.shape[0], PAIR_LEN)).reshape(tok_rows)
        token_weight = (token_weight * (chosen_mask - rejected_mask).astype(f32))[:, None]
        z = lax.axis_index("tensor").reshape(1)

        def forward(near_far, mats, deps):
            own, send = forward_tile(*near_far, mats, deps, n_x, block)
            return own, [lax.ppermute(send[s - 1], "dp", x_shift(s)) for s in range(1, n_x)]

        def gates(q, terms, deps, start=0, count=n_blocks):
            return gate_tile(*terms, grad_hidden, token_weight[begins[q]:begins[q] + sizes[q]], deps, block,
                             begins[q], start, count)

        def both_terms(own, got):
            return [[(a, m) for a in [own] + got] for m in range(2)]

        def exchange(mine):
            return [mine] + [lax.ppermute(mine, "dp", x_shift(-s)) for s in range(1, n_x)]

        def rows_of(q, n=1):
            return tokens[begins[q]:begins[q + n - 1] + sizes[q + n - 1]]

        def routed(a):
            return lax.ppermute(a, ("tensor", "dp"), route)

        column = n_tensor == SHORT
        mats = [(gate_weight, swap(gate_weight)), (up_weight, swap(up_weight))]
        weights = [pair[c] for c in range(CORES) for pair in mats]
        t0, t1 = gather_column(routed(rows_of(0, 2)), z, [(0, sizes[0]), (sizes[0], sizes[1])])
        r2 = routed(rows_of(2))
        own0, got0 = forward(t0, mats, [])
        r3 = routed(after(rows_of(3), [own0]))
        hidden0, mine0 = gates(0, both_terms(own0, got0), [])
        grads0 = exchange(mine0)
        t2, = gather_column(after(r2, [mine0]), z, [(0, sizes[2])])
        own1, got1 = forward(t1, mats, [mine0])
        own2, got2 = forward(t2, mats, [own1] + grads0[1:])
        t3, = gather_column(after(r3, [t2[0]]), z, [(0, sizes[3])])
        hidden1, mine1 = gates(1, both_terms(own1, got1), [own2])
        grads1 = exchange(mine1)

        def token_grads(grads, deps, before=None, start=0, count=n_blocks, final=True, split=False):
            return token_grad_tile(
                [[g] for g in grads], weights, before, deps, z, n_x, n_tensor, block, start, count, final, split)

        both0, *sums0 = token_grads(grads0, [mine1])
        swapped0 = swap(both0)
        near_t, far_order = order_tokens([[t0], [t1], [t2], [t3]], n_x, [both0])
        far_t = transposed(swap(far_order))
        own3, got3 = forward(t3, mats, [near_t] + got2)
        hidden2, mine2 = gates(2, both_terms(own2, got2), [own3] + grads1[1:])
        grads2 = exchange(mine2)
        hidden3, grads3 = [], []
        deps = [mine2]
        start = 0
        for count in last_split:
            h, mine = gates(3, both_terms(own3, got3), deps, start, count)
            hidden3.append(h)
            grads3.append((exchange(mine), start, count))
            deps = [mine]
            start += count
        deps += [far_t, swapped0]
        both1, *sums1 = token_grads(grads1, deps)
        swapped1 = swap(both1)
        deps = [both1]
        both2, *sums2 = token_grads(grads2, deps)
        swapped2 = swap(both2)
        done = [reduce_column([sums0[0], sums1[0]])]
        deps = [both2]
        before = None
        both3s = []
        for k, (grads, start, count) in enumerate(grads3):
            both3, *sums3 = token_grads(grads, deps, before, start, count, k == len(grads3) - 1)
            before = sums3[0]
            deps = [both3]
            both3s.append((grads, [swap(g) for g in grads], start, count))
        segments = []
        for start, count in FINAL if column and sum(c for _, c in FINAL) == n_blocks else [(0, n_blocks)]:
            for both3, swapped3, at, n in both3s:
                first, stop = max(start, at), min(start + count, at + n)
                if first < stop:
                    segments.append(((first, stop - first), [
                        [(both0, first), (both1, first), (both2, first)] + [(g, first - at) for g in both3],
                        [(swapped0, first), (swapped1, first), (swapped2, first)] + [(g, first - at) for g in swapped3]]))
        outs = weight_grad_tile([near_t, far_t], width, block, deps + done, segments[:1])
        done.append(reduce_column([sums2[0], sums3[0]]))
        out1 = send_home(done[0][sizes[0]:])
        rest = jnp.concatenate([after(done[0][:sizes[0]], [outs[0]]), done[1]], axis=0)
        outs = weight_grad_tile([near_t, far_t], width, block, [out1], segments[1:], outs)
        rest = send_home(rest)
        out = jnp.concatenate([rest[:sizes[0]], out1, rest[sizes[0]:]], axis=0)
        hidden = jnp.concatenate([hidden0, hidden1, hidden2, jnp.concatenate(hidden3, axis=1)], axis=0)
        return (hidden, out, outs[0], outs[1])

    return local


def solution(mesh):
    in_specs = (
        P(("group", "dp"), "tensor"),
        P("dp", "tensor"),
        P("dp", "tensor"),
        P(("group", "dp"), "tensor"),
        P(("group", "dp")),
        P(("group", "dp")),
        P(("group", "dp")),
    )
    out_specs = (P(("group", "dp"), "tensor"),) * 4
    local = make_local(mesh.shape["tensor"], mesh.shape["dp"])
    return jax.shard_map(local, mesh=mesh, in_specs=in_specs, out_specs=out_specs, check_vma=False)
```
